32 devices in a mesh: groups: 2 (over y), tm: 16 (over z, x, core).
Axes of the slice: x: 2, y: 2, z: 4, core: 2. Of those that a mesh axis runs over, the one named last changes fastest.
Arguments:
- unit_ids: int32 [24576], P(('groups', 'tm')), parts along dimension 0, may hold values from 0 to 999
- durations: int32 [24576], P(('groups', 'tm')), parts along dimension 0, may hold values from 1 to 8, 24576 in all
- unit_table: bfloat16 [1000, 128], replicated, may hold values from -6 to 6
- pre_weight: bfloat16 [384, 512], replicated, may hold values from -0.3125 to 0.3125
- up_weight: bfloat16 [512, 1280], replicated, may hold values from -0.25 to 0.25
- post_weight: float32 [256], replicated, may hold values from -0.375 to 0.375
- disc_taps: float32 [5, 5, 32], replicated, may hold values from -2.5 to 2.5
- disc_out: float32 [5, 32], replicated, may hold values from -1 to 1
Outputs:
- waveform: float32 [245760], P(('groups', 'tm')), parts along dimension 0
- wave_grad: float32 [245760], P(('groups', 'tm')), parts along dimension 0
- grad_pre: float32 [768, 512], P(('groups', 'tm')), parts along dimension 0
- grad_up: float32 [1024, 1280], P(('groups', 'tm')), parts along dimension 0
The draws below stay inside these ranges and needn't reach their ends.
There are 2 independent parts, one for each index of `groups`. The reference program is written for one: setup_inputs(seed, part) draws one part's arguments, and reference() takes and returns one part's arrays. A program takes and returns all parts, laid end to end along the dimension named above; an argument that names none is the same for every part. Nothing has to cross between parts.
Inputs may be any that keep to these rules, and one draw needn't show every extreme that they name: durations sum to 24576 in each utterance batch (index of groups).
All inputs are finite; a program needn't handle non-finite values.
Results may differ from the reference program's by a relative error of at most 0.0055.
Values sent between devices are 32-bit elements; how exact they have to be, the bound alone decides.
A program may use at most 128 MiB of HBM per device.

```python
import math
import jax
import jax.numpy as jnp
import numpy as np
from jax import lax

E = 128
D = 512
VOCAB = 1000
C = 256
UP = 5
NPER = 5
KD = 5
DISC_CH = 32
UNITS = 12288
FRAMES = 24576
SAMPLES = 122880


def with_ends(values, stream_key, smallest, largest):
    longest = values.shape.index(max(values.shape))
    spots = []
    for shift in (0, 1):
        where = [jax.random.randint(jax.random.fold_in(stream_key, axis), (), 0, length) for axis, length in enumerate(values.shape)]
        where[longest] = (where[longest] + shift) % values.shape[longest]
        spots.append(tuple(where))
    return values.at[spots[0]].set(smallest).at[spots[1]].set(largest)


def length_profile(number_of, total, limit, slope):
    loads = [(1 << 20) // math.isqrt(standing ** slope) + 1 for standing in range(2, number_of + 1)]
    rest, counts = total - limit - (number_of - 1), [1] * (number_of - 1)
    while rest > 0:
        candidates = [i for i in range(number_of - 1) if counts[i] < limit]
        whole, budget = sum([loads[i] for i in candidates]), rest
        for i in candidates:
            addition = min(limit - counts[i], max(1, budget * loads[i] // whole), rest)
            counts[i] = counts[i] + addition
            rest = rest - addition
    return np.array([limit] + counts)


def ragged_sizes(key, amount, total, reach, lean):
    if amount == 2:
        one = jax.random.randint(key, (), max(1, total - reach), min(reach, total - 1) + 1)
        return jnp.stack([one, total - one])
    lengths = jnp.asarray(length_profile(amount, total, reach, lean), jnp.int32)
    pairs = (amount - 1) // 2
    source_of, taker = lengths[1:1 + 2 * pairs:2], lengths[2:2 + 2 * pairs:2]
    margin = jnp.minimum(source_of - 1, reach - taker)
    passed = jax.random.randint(jax.random.fold_in(key, 1), (pairs,), 0, 1 << 20) % (margin + 1)
    lengths = lengths.at[1:1 + 2 * pairs:2].set(source_of - passed).at[2:2 + 2 * pairs:2].set(taker + passed)
    return lengths[jax.random.permutation(jax.random.fold_in(key, 2), amount)]


def scatter_about(own_key, dims, scale, limit, kind=jnp.bfloat16):
    drawn = jax.random.normal(own_key, dims, jnp.float32) * scale
    return jnp.minimum(jnp.maximum(drawn, -limit), limit).astype(kind)


def setup_inputs(seed: int = 0, part: int = 0) -> dict:
    seeds = jax.random.split(jax.random.key(seed), 9)
    part_splits = jax.random.split(jax.random.fold_in(seeds[8], part), 9)
    return {
        "unit_ids": with_ends(jax.random.randint(part_splits[0], (UNITS,), 0, VOCAB), jax.random.fold_in(part_splits[0], 1), 0, VOCAB - 1).astype(jnp.int32),
        "durations": ragged_sizes(part_splits[1], UNITS, FRAMES, 8, 2).astype(jnp.int32),
        "unit_table": scatter_about(seeds[2], (VOCAB, E), 1.0, 6.0),
        "pre_weight": scatter_about(seeds[3], (3 * E, D), (3 * E) ** -0.5, 0.3125),
        "up_weight": scatter_about(seeds[4], (D, UP * C), D ** -0.5, 0.25),
        "post_weight": scatter_about(seeds[5], (C,), C ** -0.5, 0.375, jnp.float32),
        "disc_taps": scatter_about(seeds[6], (NPER, KD, DISC_CH), KD ** -0.5, 2.5, jnp.float32),
        "disc_out": scatter_about(seeds[7], (NPER, DISC_CH), DISC_CH ** -0.5, 1.0, jnp.float32),
    }


period_list = (2, 3, 5, 7, 11)
log_two = 0.6931471805599453


def leaky_relu(v):
    return 0.1 * v + 0.9 * (jax.nn.softplus(v) - log_two)


def leaky_slope(v):
    return 0.1 + 0.9 * jax.nn.sigmoid(v)


def reference(unit_ids, durations, unit_table, pre_weight, up_weight, post_weight, disc_taps, disc_out):
    highest = lax.Precision.HIGHEST
    unit_ends = jnp.cumsum(durations).astype(jnp.int32)
    positions = jnp.arange(FRAMES, dtype=jnp.int32)
    owner_idx = jnp.searchsorted(unit_ends, positions, side="right").astype(jnp.int32)
    frames = unit_table[unit_ids[owner_idx]]
    zero_row = jnp.zeros((1, E), jnp.bfloat16)
    padded = jnp.concatenate([zero_row, frames, zero_row], axis=0)
    frame_window = jnp.concatenate([padded[:-2], padded[1:-1], padded[2:]], axis=1)
    pre_out = jnp.dot(frame_window, pre_weight, preferred_element_type=jnp.float32).astype(jnp.bfloat16)
    pre_float = pre_out.astype(jnp.float32)
    pre_act = leaky_relu(pre_float).astype(jnp.bfloat16)
    up_out = jnp.dot(pre_act, up_weight, preferred_element_type=jnp.float32).astype(jnp.bfloat16)
    up_float = up_out.reshape(SAMPLES, C).astype(jnp.float32)
    up_act = leaky_relu(up_float)
    waveform = jnp.tanh(jnp.dot(up_act, post_weight, precision=highest))
    rim_width = 4 * max(period_list)
    extended = jnp.concatenate([waveform, jnp.zeros((rim_width,), jnp.float32)])
    wave_grad = jnp.zeros((SAMPLES,), jnp.float32)
    for r, period in enumerate(period_list):
        tap_rows = jnp.stack([extended[k * period:k * period + SAMPLES] for k in range(KD)])
        disc_pre = jnp.dot(disc_taps[r].T, tap_rows, precision=highest)
        scores = jnp.dot(disc_out[r], leaky_relu(disc_pre), precision=highest)
        errors = scores - 1.0
        adjoint = jnp.dot(disc_taps[r], disc_out[r][:, None] * leaky_slope(disc_pre), precision=highest) * errors[None, :]
        for k in range(KD):
            wave_grad = wave_grad + jnp.pad(adjoint[k], (k * period, 0))[:SAMPLES]
    tanh_grad = wave_grad * (1.0 - waveform * waveform)
    up_grad = (tanh_grad[:, None] * post_weight[None, :] * leaky_slope(up_float)).astype(jnp.bfloat16)
    up_grad = up_grad.reshape(FRAMES, UP * C)
    mean_scale = 1.0 / SAMPLES
    grad_up = jnp.dot(pre_act.T, up_grad, preferred_element_type=jnp.float32) * mean_scale
    hidden_grad = jnp.dot(up_grad, up_weight.T, preferred_element_type=jnp.float32)
    pre_grad = (hidden_grad * leaky_slope(pre_float)).astype(jnp.bfloat16)
    grad_pre = jnp.dot(frame_window.T, pre_grad, preferred_element_type=jnp.float32) * mean_scale
    return (waveform, wave_grad, grad_pre, grad_up)
```

```python
import functools

import jax
import jax.numpy as jnp
from jax import lax
from jax.experimental import pallas as pl
from jax.experimental.pallas import tpu as pltpu
from jax.sharding import PartitionSpec as P

C = 256
UP = 5
KD = 5
F_DEV = 1536
HALO = 16
EXT = F_DEV + 2 * HALO

period_list = (2, 3, 5, 7, 11)
log_two = 0.6931471805599453
MESH = pl.DeviceIdType.MESH
VMEM = pltpu.VMEM


def leaky_relu(v):
    return 0.1 * v + 0.9 * (jax.nn.softplus(v) - log_two)


def leaky_slope(v):
    return 0.1 + 0.9 * jax.nn.sigmoid(v)


def left_product(left, right):
    return lax.dot_general(
        left, right, (((0,), (0,)), ((), ())), preferred_element_type=jnp.float32
    )


def at_device(group, index):
    return (group, index)


def gather_kernel(n, x_ref, o_ref, send_sem, recv_sem):
    group = lax.axis_index("groups")
    me = lax.axis_index("tm")
    barrier = pltpu.get_barrier_semaphore()

    def greet(i, carry):
        pl.semaphore_signal(
            barrier, inc=1, device_id=at_device(group, (me + i) % n), device_id_type=MESH
        )
        return carry

    lax.fori_loop(1, n, greet, 0)
    pl.semaphore_wait(barrier, n - 1)

    def copy_to(i):
        return pltpu.make_async_remote_copy(
            src_ref=x_ref,
            dst_ref=o_ref.at[me],
            send_sem=send_sem.at[i],
            recv_sem=recv_sem.at[i],
            device_id=at_device(group, (me + i) % n),
            device_id_type=MESH,
        )

    def copy_from(i):
        source = (me + n - i) % n
        return pltpu.make_async_remote_copy(
            src_ref=x_ref,
            dst_ref=o_ref.at[source],
            send_sem=send_sem.at[i],
            recv_sem=recv_sem.at[i],
            device_id=at_device(group, (me + i) % n),
            device_id_type=MESH,
        )

    def send(i, carry):
        copy_to(i).start()
        return carry

    lax.fori_loop(1, n, send, 0)
    o_ref[me] = x_ref[...]

    def finish(i, carry):
        copy_from(i).wait()
        return carry

    lax.fori_loop(1, n, finish, 0)


def gather_all(x, n):
    return pl.pallas_call(
        functools.partial(gather_kernel, n),
        out_shape=jax.ShapeDtypeStruct((n,) + x.shape, x.dtype),
        in_specs=[pl.BlockSpec(memory_space=VMEM)],
        out_specs=pl.BlockSpec(memory_space=VMEM),
        scratch_shapes=[pltpu.SemaphoreType.DMA((n,)), pltpu.SemaphoreType.DMA((n,))],
        compiler_params=pltpu.CompilerParams(collective_id=0, has_side_effects=True),
    )(x)


def stream_plan(nbits, order):
    left = list(range(nbits))[::-1]
    plan = []
    for bit in order:
        place = left.index(bit)
        plan.append((bit, 2**place, 2 ** (len(left) - place - 1)))
        left.remove(bit)
    return plan


def scatter_kernel(n, nbits, plans, targets, *refs):
    count = len(plans)
    ins, refs = refs[:count], refs[count:]
    outs, refs = refs[:2], refs[2:]
    held, refs = refs[: count * (nbits - 1)], refs[count * (nbits - 1) :]
    landed, refs = refs[: count * nbits], refs[count * nbits :]
    send_sem, recv_sem = refs
    group = lax.axis_index("groups")
    me = lax.axis_index("tm")
    bits = [(me // 2**b) % 2 for b in range(nbits)]
    mates = [me + (1 - 2 * bits[b]) * 2**b for b in range(nbits)]
    barrier = pltpu.get_barrier_semaphore()
    for b in range(nbits):
        pl.semaphore_signal(
            barrier, inc=1, device_id=at_device(group, mates[b]), device_id_type=MESH
        )
    pl.semaphore_wait(barrier, nbits)

    def source(s, t):
        return ins[s] if t == 0 else held[s * (nbits - 1) + t - 1]

    def copy(s, t):
        bit = plans[s][t][0]
        return pltpu.make_async_remote_copy(
            src_ref=source(s, t).at[:, 1 - bits[bit]],
            dst_ref=landed[s * nbits + t],
            send_sem=send_sem.at[s * nbits + t],
            recv_sem=recv_sem.at[s * nbits + t],
            device_id=at_device(group, mates[bit]),
            device_id_type=MESH,
        )

    for s in range(count):
        copy(s, 0).start()
    for t in range(nbits):
        for s in range(count):
            copy(s, t).wait_recv()
            bit, hi, lo = plans[s][t]
            here, there = source(s, t), landed[s * nbits + t]
            if t < nbits - 1:
                _, _, next_lo = plans[s][t + 1]
                for i in range(hi * lo):
                    total = here[i // lo, bits[bit], i % lo] + there[i // lo, i % lo]
                    held[s * (nbits - 1) + t][
                        i // (2 * next_lo), (i // next_lo) % 2, i % next_lo
                    ] = total
                copy(s, t + 1).start()
            else:
                which, column, width = targets[s]
                outs[which][:, column : column + width] = here[0, bits[bit], 0] + there[0, 0]
    for t in range(nbits):
        for s in range(count):
            copy(s, t).wait_send()


def scatter_sums(term_pre, terms_up, n):
    nbits = n.bit_length() - 1
    first = tuple(range(nbits))
    second = (0,) + tuple(range(2, nbits)) + (1,)
    arrays = [term_pre] + terms_up
    orders = [first] + [second, first, second, first, second]
    plans = [stream_plan(nbits, order) for order in orders]
    ins, held, landed = [], [], []
    for x, plan in zip(arrays, plans):
        rows, width = x.shape[0] // n, x.shape[1]
        _, hi, lo = plan[0]
        ins.append(x.reshape(hi, 2, lo, rows, width))
        for t, (_, hi, lo) in enumerate(plan):
            if t > 0:
                held.append(VMEM((hi, 2, lo, rows, width), jnp.float32))
            landed.append(VMEM((hi, lo, rows, width), jnp.float32))
    targets = [(0, 0, term_pre.shape[1])] + [(1, C * j, C) for j in range(len(terms_up))]
    sems = len(arrays) * nbits
    return pl.pallas_call(
        functools.partial(scatter_kernel, n, nbits, plans, targets),
        out_shape=[
            jax.ShapeDtypeStruct((term_pre.shape[0] // n, term_pre.shape[1]), jnp.float32),
            jax.ShapeDtypeStruct((terms_up[0].shape[0] // n, C * len(terms_up)), jnp.float32),
        ],
        in_specs=[pl.BlockSpec(memory_space=VMEM)] * len(ins),
        out_specs=[pl.BlockSpec(memory_space=VMEM)] * 2,
        scratch_shapes=held
        + landed
        + [pltpu.SemaphoreType.DMA((sems,)), pltpu.SemaphoreType.DMA((sems,))],
        compiler_params=pltpu.CompilerParams(
            collective_id=1, has_side_effects=True, vmem_limit_bytes=48 << 20
        ),
    )(*ins)


def frame_rows_of(gathered, unit_table, total_frames):
    n = gathered.shape[0]
    all_ids = gathered[:, 0].reshape(-1)
    dur_rows = gathered[:, 1].reshape(n, -1)
    row_units = dur_rows.shape[1]
    unit_iota = jnp.arange(row_units, dtype=jnp.int32)
    upper = (unit_iota[:, None] <= unit_iota[None, :]).astype(jnp.bfloat16)
    within = jnp.dot(dur_rows.astype(jnp.bfloat16), upper, preferred_element_type=jnp.float32)
    row_total = within[:, row_units - 1]
    offsets = jnp.cumsum(row_total) - row_total
    unit_ends = (within + offsets[:, None]).reshape(-1).astype(jnp.int32)
    width = EXT + 2
    positions = lax.axis_index("tm") * F_DEV - HALO - 1 + jnp.arange(width, dtype=jnp.int32)
    far_end = jnp.full((width,), total_frames + width, jnp.int32)
    ends_padded = jnp.concatenate([unit_ends, far_end])
    ids_padded = jnp.concatenate([all_ids, jnp.zeros((width + 1,), jnp.int32)])
    first_unit = jnp.sum((unit_ends <= positions[0]).astype(jnp.int32))
    window_ends = lax.dynamic_slice_in_dim(ends_padded, first_unit, width)
    window_ids = lax.dynamic_slice_in_dim(ids_padded, first_unit, width + 1)
    local_unit = jnp.sum((window_ends[None, :] <= positions[:, None]).astype(jnp.int32), axis=1)
    slot_iota = jnp.arange(width + 1, dtype=jnp.int32)
    picks = local_unit[:, None] == slot_iota[None, :]
    frame_ids = jnp.sum(jnp.where(picks, window_ids[None, :], 0), axis=1)
    inside = (positions >= 0) & (positions < total_frames)
    frame_ids = jnp.where(inside, frame_ids, -1)
    vocab_iota = jnp.arange(unit_table.shape[0], dtype=jnp.int32)
    one_hot = (frame_ids[:, None] == vocab_iota[None, :]).astype(jnp.bfloat16)
    return jnp.dot(one_hot, unit_table, preferred_element_type=jnp.float32).astype(jnp.bfloat16)


def per_device(
    unit_ids, durations, unit_table, pre_weight, up_weight, post_weight, disc_taps, disc_out
):
    highest = lax.Precision.HIGHEST
    devices = lax.axis_size("tm")
    total_frames = F_DEV * devices
    total_samples = UP * total_frames
    gathered = gather_all(jnp.stack([unit_ids.reshape(-1, 128), durations.reshape(-1, 128)]), devices)
    frame_rows = frame_rows_of(gathered, unit_table, total_frames)
    frame_window = jnp.concatenate([frame_rows[:-2], frame_rows[1:-1], frame_rows[2:]], axis=1)
    pre_out = jnp.dot(frame_window, pre_weight, preferred_element_type=jnp.float32).astype(
        jnp.bfloat16
    )
    pre_act = leaky_relu(pre_out.astype(jnp.float32)).astype(jnp.bfloat16)
    up_out = jnp.dot(pre_act, up_weight, preferred_element_type=jnp.float32).astype(jnp.bfloat16)
    waves = []
    for j in range(UP):
        up_act = leaky_relu(up_out[:, C * j : C * (j + 1)].astype(jnp.float32))
        waves.append(jnp.sum(up_act * post_weight[None, :], axis=1))
    wave = jnp.tanh(jnp.stack(waves, axis=1)).reshape(-1)
    rim = UP * HALO
    local_samples = UP * F_DEV
    where = lax.axis_index("tm") * local_samples - rim + jnp.arange(UP * EXT, dtype=jnp.int32)
    wave = jnp.where((where >= 0) & (where < total_samples), wave, 0.0)
    waveform = wave[rim : rim + local_samples]
    span = local_samples + rim
    wave_grad = jnp.zeros((local_samples,), jnp.float32)
    for r, period in enumerate(period_list):
        tap_rows = jnp.stack([wave[k * period : k * period + span] for k in range(KD)])
        disc_pre = jnp.dot(disc_taps[r].T, tap_rows, precision=highest)
        scores = jnp.dot(disc_out[r], leaky_relu(disc_pre), precision=highest)
        errors = jnp.where(where[:span] >= 0, scores - 1.0, 0.0)
        adjoint = (
            jnp.dot(disc_taps[r], disc_out[r][:, None] * leaky_slope(disc_pre), precision=highest)
            * errors[None, :]
        )
        for k in range(KD):
            begin = rim - k * period
            wave_grad = wave_grad + adjoint[k, begin : begin + local_samples]
    tanh_grad = (wave_grad * (1.0 - waveform * waveform)).reshape(F_DEV, UP)
    inner = slice(HALO, HALO + F_DEV)
    act = pre_act[inner]
    hidden_grad = jnp.zeros((F_DEV, up_weight.shape[0]), jnp.float32)
    terms_up, grads = [], []
    for j in range(UP):
        slope = leaky_slope(up_out[inner, C * j : C * (j + 1)].astype(jnp.float32))
        grad = (tanh_grad[:, j : j + 1] * post_weight[None, :] * slope).astype(jnp.bfloat16)
        terms_up.append(left_product(act, grad))
        grads.append(grad)
    up_grad = jnp.concatenate(grads, axis=1)
    hidden_grad = jnp.dot(up_grad, up_weight.T, preferred_element_type=jnp.float32)
    pre_grad = (hidden_grad * leaky_slope(pre_out[inner].astype(jnp.float32))).astype(jnp.bfloat16)
    term_pre = left_product(frame_window[inner], pre_grad)
    grad_pre, grad_up = scatter_sums(term_pre, terms_up, devices)
    mean_scale = 1.0 / total_samples
    return (waveform, wave_grad, grad_pre * mean_scale, grad_up * mean_scale)


def solution(mesh):
    in_specs = (P(("groups", "tm")), P(("groups", "tm")), P(), P(), P(), P(), P(), P())
    out_specs = (
        P(("groups", "tm")),
        P(("groups", "tm")),
        P(("groups", "tm"), None),
        P(("groups", "tm"), None),
    )
    return jax.shard_map(
        per_device, mesh=mesh, in_specs=in_specs, out_specs=out_specs, check_vma=False
    )
```

```python
import functools

import jax
import jax.numpy as jnp
import numpy as np
from jax import lax
from jax.experimental import pallas as pl
from jax.experimental.pallas import tpu as pltpu
from jax.sharding import PartitionSpec as P

C = 256
UP = 5
KD = 5
F_DEV = 1536
HALO = 16
EXT = F_DEV + 2 * HALO
FRONT = 224
BACK = 256
LANES = 1664
CHUNK = 128
TURNS = 10
PAIRS = 32
CHANNELS = 160

period_list = (2, 3, 5, 7, 11)
log_two = 0.6931471805599453
MESH = pl.DeviceIdType.MESH
VMEM = pltpu.VMEM


def leaky_relu(v):
    return 0.1 * v + 0.9 * (jnp.maximum(v, 0.0) + jnp.log(1.0 + jnp.exp(-jnp.abs(v))) - log_two)


def leaky_slope(v):
    return 0.55 + 0.45 * jnp.tanh(0.5 * v)


def left_product(left, right):
    return lax.dot_general(
        left, right, (((0,), (0,)), ((), ())), preferred_element_type=jnp.float32
    )


def at_device(group, index):
    return (group, index)


def gather_kernel(n, x_ref, o_ref, send_sem, recv_sem):
    group = lax.axis_index("groups")
    me = lax.axis_index("tm")
    barrier = pltpu.get_barrier_semaphore()

    def greet(i, carry):
        pl.semaphore_signal(
            barrier, inc=1, device_id=at_device(group, (me + i) % n), device_id_type=MESH
        )
        return carry

    lax.fori_loop(1, n, greet, 0)
    pl.semaphore_wait(barrier, n - 1)

    def copy_to(i):
        return pltpu.make_async_remote_copy(
            src_ref=x_ref,
            dst_ref=o_ref.at[me],
            send_sem=send_sem.at[i],
            recv_sem=recv_sem.at[i],
            device_id=at_device(group, (me + i) % n),
            device_id_type=MESH,
        )

    def copy_from(i):
        source = (me + n - i) % n
        return pltpu.make_async_remote_copy(
            src_ref=x_ref,
            dst_ref=o_ref.at[source],
            send_sem=send_sem.at[i],
            recv_sem=recv_sem.at[i],
            device_id=at_device(group, (me + i) % n),
            device_id_type=MESH,
        )

    def send(i, carry):
        copy_to(i).start()
        return carry

    lax.fori_loop(1, n, send, 0)
    o_ref[me] = x_ref[...]

    def finish(i, carry):
        copy_from(i).wait()
        return carry

    lax.fori_loop(1, n, finish, 0)


def gather_all(x, n):
    return pl.pallas_call(
        functools.partial(gather_kernel, n),
        out_shape=jax.ShapeDtypeStruct((n,) + x.shape, x.dtype),
        in_specs=[pl.BlockSpec(memory_space=VMEM)],
        out_specs=pl.BlockSpec(memory_space=VMEM),
        scratch_shapes=[pltpu.SemaphoreType.DMA((n,)), pltpu.SemaphoreType.DMA((n,))],
        compiler_params=pltpu.CompilerParams(collective_id=0, has_side_effects=True),
    )(x)


def stream_plan(nbits, order):
    left = list(range(nbits))[::-1]
    plan = []
    for bit in order:
        place = left.index(bit)
        plan.append((bit, 2**place, 2 ** (len(left) - place - 1)))
        left.remove(bit)
    return plan


def scatter_kernel(n, nbits, plans, targets, *refs):
    count = len(plans)
    ins, refs = refs[:count], refs[count:]
    outs, refs = refs[:2], refs[2:]
    held, refs = refs[: count * (nbits - 1)], refs[count * (nbits - 1) :]
    landed, refs = refs[: count * nbits], refs[count * nbits :]
    send_sem, recv_sem = refs
    group = lax.axis_index("groups")
    me = lax.axis_index("tm")
    bits = [(me // 2**b) % 2 for b in range(nbits)]
    mates = [me + (1 - 2 * bits[b]) * 2**b for b in range(nbits)]
    barrier = pltpu.get_barrier_semaphore()
    for b in range(nbits):
        pl.semaphore_signal(
            barrier, inc=1, device_id=at_device(group, mates[b]), device_id_type=MESH
        )
    pl.semaphore_wait(barrier, nbits)

    def source(s, t):
        return ins[s] if t == 0 else held[s * (nbits - 1) + t - 1]

    def copy(s, t):
        bit = plans[s][t][0]
        return pltpu.make_async_remote_copy(
            src_ref=source(s, t).at[:, 1 - bits[bit]],
            dst_ref=landed[s * nbits + t],
            send_sem=send_sem.at[s * nbits + t],
            recv_sem=recv_sem.at[s * nbits + t],
            device_id=at_device(group, mates[bit]),
            device_id_type=MESH,
        )

    for s in range(count):
        copy(s, 0).start()
    for t in range(nbits):
        for s in range(count):
            copy(s, t).wait_recv()
            bit, hi, lo = plans[s][t]
            here, there = source(s, t), landed[s * nbits + t]
            if t < nbits - 1:
                _, _, next_lo = plans[s][t + 1]
                for i in range(hi * lo):
                    total = here[i // lo, bits[bit], i % lo] + there[i // lo, i % lo]
                    held[s * (nbits - 1) + t][
                        i // (2 * next_lo), (i // next_lo) % 2, i % next_lo
                    ] = total
                copy(s, t + 1).start()
            else:
                which, column, width = targets[s]
                outs[which][:, column : column + width] = here[0, bits[bit], 0] + there[0, 0]
    for t in range(nbits):
        for s in range(count):
            copy(s, t).wait_send()


def scatter_sums(term_pre, terms_up, n):
    nbits = n.bit_length() - 1
    first = tuple(range(nbits))
    second = (0,) + tuple(range(2, nbits)) + (1,)
    arrays = [term_pre] + terms_up
    orders = [first] + [second, first, second, first, second]
    plans = [stream_plan(nbits, order) for order in orders]
    ins, held, landed = [], [], []
    for x, plan in zip(arrays, plans):
        rows, width = x.shape[0] // n, x.shape[1]
        _, hi, lo = plan[0]
        ins.append(x.reshape(hi, 2, lo, rows, width))
        for t, (_, hi, lo) in enumerate(plan):
            if t > 0:
                held.append(VMEM((hi, 2, lo, rows, width), jnp.float32))
            landed.append(VMEM((hi, lo, rows, width), jnp.float32))
    targets = [(0, 0, term_pre.shape[1])] + [(1, C * j, C) for j in range(len(terms_up))]
    sems = len(arrays) * nbits
    return pl.pallas_call(
        functools.partial(scatter_kernel, n, nbits, plans, targets),
        out_shape=[
            jax.ShapeDtypeStruct((term_pre.shape[0] // n, term_pre.shape[1]), jnp.float32),
            jax.ShapeDtypeStruct((terms_up[0].shape[0] // n, C * len(terms_up)), jnp.float32),
        ],
        in_specs=[pl.BlockSpec(memory_space=VMEM)] * len(ins),
        out_specs=[pl.BlockSpec(memory_space=VMEM)] * 2,
        scratch_shapes=held
        + landed
        + [pltpu.SemaphoreType.DMA((sems,)), pltpu.SemaphoreType.DMA((sems,))],
        compiler_params=pltpu.CompilerParams(
            collective_id=1, has_side_effects=True, vmem_limit_bytes=48 << 20
        ),
    )(*ins)


def frame_ids_of(gathered, total_frames):
    n = gathered.shape[0]
    all_ids = gathered[:, 0].reshape(-1)
    dur_rows = gathered[:, 1].reshape(n, -1)
    row_units = dur_rows.shape[1]
    unit_iota = jnp.arange(row_units, dtype=jnp.int32)
    upper = (unit_iota[:, None] <= unit_iota[None, :]).astype(jnp.bfloat16)
    within = jnp.dot(dur_rows.astype(jnp.bfloat16), upper, preferred_element_type=jnp.float32)
    row_total = within[:, row_units - 1]
    offsets = jnp.cumsum(row_total) - row_total
    unit_ends = (within + offsets[:, None]).reshape(-1).astype(jnp.int32)
    width = EXT + 2
    positions = lax.axis_index("tm") * F_DEV - HALO - 1 + jnp.arange(width, dtype=jnp.int32)
    far_end = jnp.full((width,), total_frames + width, jnp.int32)
    ends_padded = jnp.concatenate([unit_ends, far_end])
    ids_padded = jnp.concatenate([all_ids, jnp.zeros((width + 1,), jnp.int32)])
    first_unit = jnp.sum((unit_ends <= positions[0]).astype(jnp.int32))
    window_ends = lax.dynamic_slice_in_dim(ends_padded, first_unit, width)
    window_ids = lax.dynamic_slice_in_dim(ids_padded, first_unit, width + 1)
    local_unit = jnp.sum((window_ends[None, :] <= positions[:, None]).astype(jnp.int32), axis=1)
    slot_iota = jnp.arange(width + 1, dtype=jnp.int32)
    picks = local_unit[:, None] == slot_iota[None, :]
    frame_ids = jnp.sum(jnp.where(picks, window_ids[None, :], 0), axis=1)
    inside = (positions >= 0) & (positions < total_frames)
    frame_ids = jnp.where(inside, frame_ids, -1)
    spare = FRONT * (-(-width // FRONT)) - width
    return jnp.concatenate([frame_ids, jnp.full((spare,), -1, jnp.int32)])[:, None]


def tap_places():
    reads = np.zeros((UP, 5, KD, TURNS * 8), np.float32)
    adds = np.zeros((TURNS * 8, UP * PAIRS), np.float32)
    for phase in range(UP):
        for r, period in enumerate(period_list):
            for k in range(KD):
                ahead = phase + k * period
                reads[phase, r, k, (ahead // UP) * 8 + ahead % UP] = 1.0
                behind = phase - k * period
                row = (-(behind // UP)) * 8 + phase
                adds[row, (behind % UP) * PAIRS + r * KD + k] = 1.0
    return reads, adds


def halves(x):
    high = x.astype(jnp.bfloat16)
    return high, (x - high.astype(jnp.float32)).astype(jnp.bfloat16)


def disc_matrices(disc_taps, disc_out):
    reads, adds = tap_places()
    spread = jnp.sum(disc_taps[None, :, :, :, None] * reads[:, :, :, None, :], axis=2)
    high, low = halves(spread.reshape(UP * CHANNELS, TURNS * 8))
    read_matrix = jnp.concatenate([high, high, low], axis=1)
    own = jnp.asarray(np.eye(5, dtype=np.float32))
    weighted = disc_taps * disc_out[:, None, :]
    repeated = jnp.broadcast_to(disc_out[:, None, :], disc_taps.shape)
    parts = []
    for x in (weighted, repeated):
        full = (x[:, :, None, :] * own[:, None, :, None]).reshape(25, CHANNELS)
        full = jnp.concatenate([full, jnp.zeros((PAIRS - 25, CHANNELS), jnp.float32)], axis=0)
        parts.append(jnp.concatenate(halves(full), axis=0))
    add_matrix = jnp.asarray(np.concatenate([adds, adds], axis=1), jnp.bfloat16)
    return read_matrix, parts[0], parts[1], add_matrix


def split_dot(matrix, x):
    high, low = halves(x)
    both = jnp.dot(matrix, high, preferred_element_type=jnp.float32)
    rest = jnp.dot(matrix[:PAIRS], low, preferred_element_type=jnp.float32)
    return both[:PAIRS] + both[PAIRS:] + rest


def step_kernel(
    total_frames,
    ids_ref,
    table_ref,
    pre_w,
    up_w,
    post_ref,
    read_ref,
    weighted_ref,
    repeated_ref,
    add_ref,
    window_o,
    act_o,
    up_grad_o,
    pre_grad_o,
    wave_o,
    wave_grad_o,
    rows,
    window,
    pre_out,
    pre_act,
    up_out,
    columns,
    wave,
    shifted,
    sums,
):
    first_frame = lax.axis_index("tm") * F_DEV - HALO
    vocab = table_ref.shape[0]

    def embed(i, carry):
        at = pl.multiple_of(i * FRONT, FRONT)
        ids = ids_ref[pl.ds(at, FRONT), :]
        one_hot = (ids == lax.broadcasted_iota(jnp.int32, (FRONT, vocab), 1)).astype(jnp.bfloat16)
        rows[pl.ds(at, FRONT), :] = jnp.dot(
            one_hot, table_ref[...], preferred_element_type=jnp.float32
        )
        return carry

    lax.fori_loop(0, ids_ref.shape[0] // FRONT, embed, 0)

    columns[pl.ds(EXT, LANES - EXT), :] = jnp.zeros((LANES - EXT, 128), jnp.float32)
    lane = lax.broadcasted_iota(jnp.int32, (FRONT, 128), 1)
    for i in range(EXT // FRONT):
        at = i * FRONT
        taps = [rows[at + k : at + k + FRONT, :].astype(jnp.bfloat16) for k in range(3)]
        win = jnp.concatenate(taps, axis=1)
        window[at : at + FRONT, :] = win
        pre = jnp.dot(win, pre_w[...], preferred_element_type=jnp.float32).astype(jnp.bfloat16)
        pre_out[at : at + FRONT, :] = pre
        act = leaky_relu(pre.astype(jnp.float32)).astype(jnp.bfloat16)
        pre_act[at : at + FRONT, :] = act
        column = jnp.zeros((FRONT, 128), jnp.float32)
        for j in range(UP):
            up = jnp.dot(
                act, up_w[:, C * j : C * (j + 1)], preferred_element_type=jnp.float32
            ).astype(jnp.bfloat16)
            up_out[at : at + FRONT, C * j : C * (j + 1)] = up
            terms = leaky_relu(up.astype(jnp.float32)) * post_ref[...]
            column = jnp.where(lane == j, jnp.sum(terms, axis=1, keepdims=True), column)
        columns[at : at + FRONT, :] = column

    frame = lax.broadcasted_iota(jnp.int32, (8, LANES), 1) + first_frame
    for b in range(LANES // 128):
        at = 128 * b
        wave[:, at : at + 128] = columns[at : at + 128, :].T[:8, :]
    inside = (frame >= 0) & (frame < total_frames)
    signal = jnp.where(inside, jnp.tanh(wave[...]), 0.0)
    wave[...] = signal
    depth = TURNS * 8
    for q in range(0, TURNS, 2):
        turned = [signal if t == 0 else pltpu.roll(signal, LANES - t, 1) for t in (q, q + 1)]
        high, low = halves(jnp.concatenate(turned, axis=0))
        shifted[8 * q : 8 * q + 16, :] = high
        shifted[depth + 8 * q : depth + 8 * q + 16, :] = low
        shifted[2 * depth + 8 * q : 2 * depth + 8 * q + 16, :] = high

    chunk_lane = lax.broadcasted_iota(jnp.int32, (PAIRS, CHUNK), 1)

    def judge(i, carry):
        at = pl.multiple_of(i * CHUNK, CHUNK)
        real = chunk_lane + (at + first_frame) >= 0
        taps = shifted[:, pl.ds(at, CHUNK)]
        highs, lows = [], []
        for j in range(UP):
            pre = jnp.dot(
                read_ref[CHANNELS * j : CHANNELS * (j + 1), :],
                taps,
                preferred_element_type=jnp.float32,
            )
            scores = split_dot(repeated_ref[...], leaky_relu(pre))
            adjoint = split_dot(weighted_ref[...], leaky_slope(pre)) * (scores - 1.0)
            high, low = halves(jnp.where(real, adjoint, 0.0))
            highs.append(high)
            lows.append(low)
        sums[:, pl.ds(at, CHUNK)] = jnp.dot(
            add_ref[...], jnp.concatenate(highs + lows, axis=0), preferred_element_type=jnp.float32
        )
        return carry

    lax.fori_loop(0, LANES // CHUNK, judge, 0)
    wave_grad = sums[0:8, :]
    for q in range(1, TURNS):
        wave_grad = wave_grad + pltpu.roll(sums[8 * q : 8 * q + 8, :], q, 1)
    wave_o[...] = signal
    wave_grad_o[...] = wave_grad
    sums[0:8, :] = wave_grad * (1.0 - signal * signal)
    for b in range(LANES // 128):
        at = 128 * b
        columns[at : at + 128, 0:8] = sums[0:8, at : at + 128].T

    for i in range(F_DEV // BACK):
        to, at = i * BACK, i * BACK + HALO
        window_o[to : to + BACK, :] = window[at : at + BACK, :]
        act_o[to : to + BACK, :] = pre_act[at : at + BACK, :]
        hidden = jnp.zeros((BACK, up_w.shape[0]), jnp.float32)
        for j in range(UP):
            slope = leaky_slope(up_out[at : at + BACK, C * j : C * (j + 1)].astype(jnp.float32))
            grad = columns[at : at + BACK, j : j + 1] * post_ref[...] * slope
            grad = grad.astype(jnp.bfloat16)
            up_grad_o[to : to + BACK, C * j : C * (j + 1)] = grad
            hidden = hidden + lax.dot_general(
                grad,
                up_w[:, C * j : C * (j + 1)],
                (((1,), (1,)), ((), ())),
                preferred_element_type=jnp.float32,
            )
        slope = leaky_slope(pre_out[at : at + BACK, :].astype(jnp.float32))
        pre_grad_o[to : to + BACK, :] = (hidden * slope).astype(jnp.bfloat16)


def step(frame_ids, unit_table, pre_weight, up_weight, post_weight, matrices, total_frames):
    width, depth = up_weight.shape[1], up_weight.shape[0]
    shape, bf16, f32 = jax.ShapeDtypeStruct, jnp.bfloat16, jnp.float32
    operands = (frame_ids, unit_table, pre_weight, up_weight, post_weight[None, :], *matrices)
    return pl.pallas_call(
        functools.partial(step_kernel, total_frames),
        out_shape=[
            shape((F_DEV, pre_weight.shape[0]), bf16),
            shape((F_DEV, depth), bf16),
            shape((F_DEV, width), bf16),
            shape((F_DEV, depth), bf16),
            shape((8, LANES), f32),
            shape((8, LANES), f32),
        ],
        in_specs=[pl.BlockSpec(memory_space=VMEM)] * len(operands),
        out_specs=[pl.BlockSpec(memory_space=VMEM)] * 6,
        scratch_shapes=[
            VMEM((frame_ids.shape[0], unit_table.shape[1]), f32),
            VMEM((EXT, pre_weight.shape[0]), bf16),
            VMEM((EXT, depth), bf16),
            VMEM((EXT, depth), bf16),
            VMEM((EXT, width), bf16),
            VMEM((LANES, 128), f32),
            VMEM((8, LANES), f32),
            VMEM((3 * TURNS * 8, LANES), bf16),
            VMEM((TURNS * 8, LANES), f32),
        ],
        compiler_params=pltpu.CompilerParams(vmem_limit_bytes=50 << 20),
    )(*operands)


def per_device(
    unit_ids, durations, unit_table, pre_weight, up_weight, post_weight, disc_taps, disc_out
):
    devices = lax.axis_size("tm")
    total_frames = F_DEV * devices
    total_samples = UP * total_frames
    matrices = disc_matrices(disc_taps, disc_out)
    gathered = gather_all(jnp.stack([unit_ids.reshape(-1, 128), durations.reshape(-1, 128)]), devices)
    frame_ids = frame_ids_of(gathered, total_frames)
    frame_window, act, up_grad, pre_grad, wave, wave_grad = step(
        frame_ids, unit_table, pre_weight, up_weight, post_weight, matrices, total_frames
    )
    terms_up = [left_product(act, up_grad[:, C * j : C * (j + 1)]) for j in range(UP)]
    term_pre = left_product(frame_window, pre_grad)
    grad_pre, grad_up = scatter_sums(term_pre, terms_up, devices)
    mean_scale = 1.0 / total_samples
    both = jnp.stack([wave, wave_grad])[:, :UP, HALO : HALO + F_DEV]
    both = both.transpose(0, 2, 1).reshape(2, -1)
    return (both[0], both[1], grad_pre * mean_scale, grad_up * mean_scale)


def solution(mesh):
    in_specs = (P(("groups", "tm")), P(("groups", "tm")), P(), P(), P(), P(), P(), P())
    out_specs = (
        P(("groups", "tm")),
        P(("groups", "tm")),
        P(("groups", "tm"), None),
        P(("groups", "tm"), None),
    )
    return jax.shard_map(
        per_device, mesh=mesh, in_specs=in_specs, out_specs=out_specs, check_vma=False
    )
```

```python
import functools

import jax
import jax.numpy as jnp
import numpy as np
from jax import lax
from jax.experimental import pallas as pl
from jax.experimental.pallas import tpu as pltpu
from jax.sharding import PartitionSpec as P

C = 256
UP = 5
KD = 5
F_DEV = 1536
HALO = 16
EXT = F_DEV + 2 * HALO
FRONT = 224
BACK = 256
LANES = 1664
CHUNK = 128
TURNS = 10
PAIRS = 32
CHANNELS = 160

period_list = (2, 3, 5, 7, 11)
log_two = 0.6931471805599453
MESH = pl.DeviceIdType.MESH
VMEM = pltpu.VMEM


def leaky_relu(v):
    return 0.1 * v + 0.9 * (jnp.maximum(v, 0.0) + jnp.log(1.0 + jnp.exp(-jnp.abs(v))) - log_two)


def leaky_slope(v):
    return 0.55 + 0.45 * jnp.tanh(0.5 * v)


def at_device(group, index):
    return (group, index)


def gather_kernel(n, x_ref, o_ref, send_sem, recv_sem):
    group = lax.axis_index("groups")
    me = lax.axis_index("tm")
    barrier = pltpu.get_barrier_semaphore()

    def greet(i, carry):
        pl.semaphore_signal(
            barrier, inc=1, device_id=at_device(group, (me + i) % n), device_id_type=MESH
        )
        return carry

    lax.fori_loop(1, n, greet, 0)
    pl.semaphore_wait(barrier, n - 1)

    def copy_to(i):
        return pltpu.make_async_remote_copy(
            src_ref=x_ref,
            dst_ref=o_ref.at[me],
            send_sem=send_sem.at[i],
            recv_sem=recv_sem.at[i],
            device_id=at_device(group, (me + i) % n),
            device_id_type=MESH,
        )

    def copy_from(i):
        source = (me + n - i) % n
        return pltpu.make_async_remote_copy(
            src_ref=x_ref,
            dst_ref=o_ref.at[source],
            send_sem=send_sem.at[i],
            recv_sem=recv_sem.at[i],
            device_id=at_device(group, (me + i) % n),
            device_id_type=MESH,
        )

    def send(i, carry):
        copy_to(i).start()
        return carry

    lax.fori_loop(1, n, send, 0)
    o_ref[me] = x_ref[...]

    def finish(i, carry):
        copy_from(i).wait()
        return carry

    lax.fori_loop(1, n, finish, 0)


def gather_all(x, n):
    return pl.pallas_call(
        functools.partial(gather_kernel, n),
        out_shape=jax.ShapeDtypeStruct((n,) + x.shape, x.dtype),
        in_specs=[pl.BlockSpec(memory_space=VMEM)],
        out_specs=pl.BlockSpec(memory_space=VMEM),
        scratch_shapes=[pltpu.SemaphoreType.DMA((n,)), pltpu.SemaphoreType.DMA((n,))],
        compiler_params=pltpu.CompilerParams(collective_id=0, has_side_effects=True),
    )(x)


def stream_plan(nbits, order):
    left = list(range(nbits))[::-1]
    plan = []
    for bit in order:
        place = left.index(bit)
        plan.append((bit, 2**place, 2 ** (len(left) - place - 1)))
        left.remove(bit)
    return plan


def stream_plans(n):
    nbits = n.bit_length() - 1
    first = tuple(range(nbits))
    second = (0,) + tuple(range(2, nbits)) + (1,)
    orders = [second, first, second, first, second, first, second]
    return nbits, [stream_plan(nbits, order) for order in orders]


class Halving:
    def __init__(self, n, outs, targets, terms, held, landed, send_sem, recv_sem):
        self.nbits, self.plans = stream_plans(n)
        self.outs, self.targets, self.terms = outs, targets, terms
        self.held, self.landed = held, landed
        self.send_sem, self.recv_sem = send_sem, recv_sem
        self.group, me = lax.axis_index("groups"), lax.axis_index("tm")
        self.bits = [(me // 2**b) % 2 for b in range(self.nbits)]
        self.mates = [me + (1 - 2 * self.bits[b]) * 2**b for b in range(self.nbits)]

    def greet(self):
        barrier = pltpu.get_barrier_semaphore()
        for mate in self.mates:
            pl.semaphore_signal(
                barrier, inc=1, device_id=at_device(self.group, mate), device_id_type=MESH
            )

    def meet(self):
        pl.semaphore_wait(pltpu.get_barrier_semaphore(), self.nbits)

    def source(self, s, t):
        return self.terms[s] if t == 0 else self.held[s * (self.nbits - 1) + t - 1]

    def copy(self, s, t):
        bit = self.plans[s][t][0]
        return pltpu.make_async_remote_copy(
            src_ref=self.source(s, t).at[:, 1 - self.bits[bit]],
            dst_ref=self.landed[s * self.nbits + t],
            send_sem=self.send_sem.at[s * self.nbits + t],
            recv_sem=self.recv_sem.at[s * self.nbits + t],
            device_id=at_device(self.group, self.mates[bit]),
            device_id_type=MESH,
        )

    def put(self, s, term):
        ref = self.terms[s]
        ref[...] = term.reshape(ref.shape)
        self.copy(s, 0).start()

    def advance(self, s, t):
        self.copy(s, t).wait_recv()
        bit, hi, lo = self.plans[s][t]
        mine = self.bits[bit]
        here, there = self.source(s, t), self.landed[s * self.nbits + t]
        if t == self.nbits - 1:
            which, column = self.targets[s]
            self.outs[which][:, column : column + C] = here[0, mine, 0] + there[0, 0]
            return
        _, _, next_lo = self.plans[s][t + 1]
        onward = self.held[s * (self.nbits - 1) + t]
        for i in range(hi * lo):
            total = here[i // lo, mine, i % lo] + there[i // lo, i % lo]
            onward[i // (2 * next_lo), (i // next_lo) % 2, i % next_lo] = total
        self.copy(s, t + 1).start()

    def finish(self):
        for t in range(self.nbits):
            for s in range(len(self.plans)):
                self.copy(s, t).wait_send()


def frame_ids_of(gathered, total_frames):
    n = gathered.shape[0]
    all_ids = gathered[:, 0].reshape(-1)
    dur_rows = gathered[:, 1].reshape(n, -1)
    row_units = dur_rows.shape[1]
    unit_iota = jnp.arange(row_units, dtype=jnp.int32)
    upper = (unit_iota[:, None] <= unit_iota[None, :]).astype(jnp.bfloat16)
    within = jnp.dot(dur_rows.astype(jnp.bfloat16), upper, preferred_element_type=jnp.float32)
    row_total = within[:, row_units - 1]
    offsets = jnp.cumsum(row_total) - row_total
    unit_ends = (within + offsets[:, None]).reshape(-1).astype(jnp.int32)
    width = EXT + 2
    positions = lax.axis_index("tm") * F_DEV - HALO - 1 + jnp.arange(width, dtype=jnp.int32)
    far_end = jnp.full((width,), total_frames + width, jnp.int32)
    ends_padded = jnp.concatenate([unit_ends, far_end])
    ids_padded = jnp.concatenate([all_ids, jnp.zeros((width + 1,), jnp.int32)])
    first_unit = jnp.sum((unit_ends <= positions[0]).astype(jnp.int32))
    window_ends = lax.dynamic_slice_in_dim(ends_padded, first_unit, width)
    window_ids = lax.dynamic_slice_in_dim(ids_padded, first_unit, width + 1)
    local_unit = jnp.sum((window_ends[None, :] <= positions[:, None]).astype(jnp.int32), axis=1)
    slot_iota = jnp.arange(width + 1, dtype=jnp.int32)
    picks = local_unit[:, None] == slot_iota[None, :]
    frame_ids = jnp.sum(jnp.where(picks, window_ids[None, :], 0), axis=1)
    inside = (positions >= 0) & (positions < total_frames)
    frame_ids = jnp.where(inside, frame_ids, -1)
    spare = FRONT * (-(-width // FRONT)) - width
    return jnp.concatenate([frame_ids, jnp.full((spare,), -1, jnp.int32)])[:, None]


def tap_places():
    reads = np.zeros((UP, 5, KD, TURNS * 8), np.float32)
    adds = np.zeros((TURNS * 8, UP * PAIRS), np.float32)
    for phase in range(UP):
        for r, period in enumerate(period_list):
            for k in range(KD):
                ahead = phase + k * period
                reads[phase, r, k, (ahead // UP) * 8 + ahead % UP] = 1.0
                behind = phase - k * period
                row = (-(behind // UP)) * 8 + phase
                adds[row, (behind % UP) * PAIRS + r * KD + k] = 1.0
    return reads, adds


def halves(x):
    high = x.astype(jnp.bfloat16)
    return high, (x - high.astype(jnp.float32)).astype(jnp.bfloat16)


def disc_matrices(disc_taps, disc_out):
    reads, adds = tap_places()
    spread = jnp.sum(disc_taps[None, :, :, :, None] * reads[:, :, :, None, :], axis=2)
    high, low = halves(spread.reshape(UP * CHANNELS, TURNS * 8))
    read_matrix = jnp.concatenate([high, high, low], axis=1)
    own = jnp.asarray(np.eye(5, dtype=np.float32))
    weighted = disc_taps * disc_out[:, None, :]
    repeated = jnp.broadcast_to(disc_out[:, None, :], disc_taps.shape)
    parts = []
    for x in (weighted, repeated):
        full = (x[:, :, None, :] * own[:, None, :, None]).reshape(25, CHANNELS)
        full = jnp.concatenate([full, jnp.zeros((PAIRS - 25, CHANNELS), jnp.float32)], axis=0)
        parts.append(jnp.concatenate(halves(full), axis=0))
    add_matrix = jnp.asarray(np.concatenate([adds, adds], axis=1), jnp.bfloat16)
    return read_matrix, parts[0], parts[1], add_matrix


def split_dot(matrix, x):
    high, low = halves(x)
    both = jnp.dot(matrix, high, preferred_element_type=jnp.float32)
    rest = jnp.dot(matrix[:PAIRS], low, preferred_element_type=jnp.float32)
    return both[:PAIRS] + both[PAIRS:] + rest


def step_kernel(
    devices,
    ids_ref,
    table_ref,
    pre_w,
    up_w,
    post_ref,
    read_ref,
    weighted_ref,
    repeated_ref,
    add_ref,
    wave_o,
    wave_grad_o,
    grad_pre_o,
    grad_up_o,
    rows,
    window,
    pre_out,
    pre_act,
    up_out,
    columns,
    wave,
    shifted,
    sums,
    up_grad,
    pre_grad,
    window_t,
    act_t,
    *stream_refs,
):
    nbits, plans = stream_plans(devices)
    count = len(plans)
    terms, stream_refs = stream_refs[:count], stream_refs[count:]
    held, stream_refs = stream_refs[: count * (nbits - 1)], stream_refs[count * (nbits - 1) :]
    landed, sems = stream_refs[: count * nbits], stream_refs[count * nbits :]
    targets = [(1, C * j) for j in range(UP)] + [(0, 0), (0, C)]
    halving = Halving(devices, (grad_pre_o, grad_up_o), targets, terms, held, landed, *sems)
    halving.greet()
    total_frames = devices * F_DEV
    first_frame = lax.axis_index("tm") * F_DEV - HALO
    vocab = table_ref.shape[0]

    def embed(i, carry):
        at = pl.multiple_of(i * FRONT, FRONT)
        ids = ids_ref[pl.ds(at, FRONT), :]
        one_hot = (ids == lax.broadcasted_iota(jnp.int32, (FRONT, vocab), 1)).astype(jnp.bfloat16)
        rows[pl.ds(at, FRONT), :] = jnp.dot(
            one_hot, table_ref[...], preferred_element_type=jnp.float32
        )
        return carry

    lax.fori_loop(0, ids_ref.shape[0] // FRONT, embed, 0)

    columns[pl.ds(EXT, LANES - EXT), :] = jnp.zeros((LANES - EXT, 128), jnp.float32)
    lane = lax.broadcasted_iota(jnp.int32, (FRONT, 128), 1)
    for i in range(EXT // FRONT):
        at = i * FRONT
        taps = [rows[at + k : at + k + FRONT, :].astype(jnp.bfloat16) for k in range(3)]
        win = jnp.concatenate(taps, axis=1)
        window[at : at + FRONT, :] = win
        pre = jnp.dot(win, pre_w[...], preferred_element_type=jnp.float32).astype(jnp.bfloat16)
        pre_out[at : at + FRONT, :] = pre
        act = leaky_relu(pre.astype(jnp.float32)).astype(jnp.bfloat16)
        pre_act[at : at + FRONT, :] = act
        column = jnp.zeros((FRONT, 128), jnp.float32)
        for j in range(UP):
            up = jnp.dot(
                act, up_w[:, C * j : C * (j + 1)], preferred_element_type=jnp.float32
            ).astype(jnp.bfloat16)
            up_out[at : at + FRONT, C * j : C * (j + 1)] = up
            terms = leaky_relu(up.astype(jnp.float32)) * post_ref[...]
            column = jnp.where(lane == j, jnp.sum(terms, axis=1, keepdims=True), column)
        columns[at : at + FRONT, :] = column

    frame = lax.broadcasted_iota(jnp.int32, (8, LANES), 1) + first_frame
    for b in range(LANES // 128):
        at = 128 * b
        wave[:, at : at + 128] = columns[at : at + 128, :].T[:8, :]
    inside = (frame >= 0) & (frame < total_frames)
    signal = jnp.where(inside, jnp.tanh(wave[...]), 0.0)
    wave[...] = signal
    depth = TURNS * 8
    for q in range(0, TURNS, 2):
        turned = [signal if t == 0 else pltpu.roll(signal, LANES - t, 1) for t in (q, q + 1)]
        high, low = halves(jnp.concatenate(turned, axis=0))
        shifted[8 * q : 8 * q + 16, :] = high
        shifted[depth + 8 * q : depth + 8 * q + 16, :] = low
        shifted[2 * depth + 8 * q : 2 * depth + 8 * q + 16, :] = high

    chunk_lane = lax.broadcasted_iota(jnp.int32, (PAIRS, CHUNK), 1)

    def judge(i, carry):
        at = pl.multiple_of(i * CHUNK, CHUNK)
        real = chunk_lane + (at + first_frame) >= 0
        taps = shifted[:, pl.ds(at, CHUNK)]
        highs, lows = [], []
        for j in range(UP):
            pre = jnp.dot(
                read_ref[CHANNELS * j : CHANNELS * (j + 1), :],
                taps,
                preferred_element_type=jnp.float32,
            )
            scores = split_dot(repeated_ref[...], leaky_relu(pre))
            adjoint = split_dot(weighted_ref[...], leaky_slope(pre)) * (scores - 1.0)
            high, low = halves(jnp.where(real, adjoint, 0.0))
            highs.append(high)
            lows.append(low)
        sums[:, pl.ds(at, CHUNK)] = jnp.dot(
            add_ref[...], jnp.concatenate(highs + lows, axis=0), preferred_element_type=jnp.float32
        )
        return carry

    lax.fori_loop(0, LANES // CHUNK, judge, 0)
    wave_grad = sums[0:8, :]
    for q in range(1, TURNS):
        wave_grad = wave_grad + pltpu.roll(sums[8 * q : 8 * q + 8, :], q, 1)
    wave_o[...] = signal
    wave_grad_o[...] = wave_grad
    sums[0:8, :] = wave_grad * (1.0 - signal * signal)
    for b in range(LANES // 128):
        at = 128 * b
        columns[at : at + 128, 0:8] = sums[0:8, at : at + 128].T

    blocks = [(i * BACK, i * BACK + HALO) for i in range(F_DEV // BACK)]
    for to, at in blocks:
        act_t[:, to : to + BACK] = pre_act[at : at + BACK, :].T
        window_t[:, to : to + BACK] = window[at : at + BACK, :].T
    halving.meet()
    for j in range(UP):
        for to, at in blocks:
            slope = leaky_slope(up_out[at : at + BACK, C * j : C * (j + 1)].astype(jnp.float32))
            grad = columns[at : at + BACK, j : j + 1] * post_ref[...] * slope
            up_grad[to : to + BACK, C * j : C * (j + 1)] = grad.astype(jnp.bfloat16)
        term = jnp.dot(
            act_t[...], up_grad[:, C * j : C * (j + 1)], preferred_element_type=jnp.float32
        )
        halving.put(j, term)
        if j > 0:
            halving.advance(j - 1, 0)
    for to, at in blocks:
        hidden = lax.dot_general(
            up_grad[to : to + BACK, :],
            up_w[...],
            (((1,), (1,)), ((), ())),
            preferred_element_type=jnp.float32,
        )
        slope = leaky_slope(pre_out[at : at + BACK, :].astype(jnp.float32))
        pre_grad[to : to + BACK, :] = (hidden * slope).astype(jnp.bfloat16)
    halving.advance(UP - 1, 0)
    for j in range(2):
        term = jnp.dot(
            window_t[...], pre_grad[:, C * j : C * (j + 1)], preferred_element_type=jnp.float32
        )
        halving.put(UP + j, term)
    halving.advance(UP, 0)
    halving.advance(UP + 1, 0)
    for t in range(1, nbits):
        for s in range(count):
            halving.advance(s, t)
    halving.finish()


def step(frame_ids, unit_table, pre_weight, up_weight, post_weight, matrices, devices):
    width, depth, span = up_weight.shape[1], up_weight.shape[0], pre_weight.shape[0]
    shape, bf16, f32 = jax.ShapeDtypeStruct, jnp.bfloat16, jnp.float32
    operands = (frame_ids, unit_table, pre_weight, up_weight, post_weight[None, :], *matrices)
    nbits, plans = stream_plans(devices)
    terms, held, landed = [], [], []
    for s, plan in enumerate(plans):
        rows = (depth if s < UP else span) // devices
        for t, (_, hi, lo) in enumerate(plan):
            (held if t > 0 else terms).append(VMEM((hi, 2, lo, rows, C), f32))
            landed.append(VMEM((hi, lo, rows, C), f32))
    return pl.pallas_call(
        functools.partial(step_kernel, devices),
        out_shape=[
            shape((8, LANES), f32),
            shape((8, LANES), f32),
            shape((span // devices, depth), f32),
            shape((depth // devices, width), f32),
        ],
        in_specs=[pl.BlockSpec(memory_space=VMEM)] * len(operands),
        out_specs=[pl.BlockSpec(memory_space=VMEM)] * 4,
        scratch_shapes=[
            VMEM((frame_ids.shape[0], unit_table.shape[1]), f32),
            VMEM((EXT, span), bf16),
            VMEM((EXT, depth), bf16),
            VMEM((EXT, depth), bf16),
            VMEM((EXT, width), bf16),
            VMEM((LANES, 128), f32),
            VMEM((8, LANES), f32),
            VMEM((3 * TURNS * 8, LANES), bf16),
            VMEM((TURNS * 8, LANES), f32),
            VMEM((F_DEV, width), bf16),
            VMEM((F_DEV, depth), bf16),
            VMEM((span, F_DEV), bf16),
            VMEM((depth, F_DEV), bf16),
            *terms,
            *held,
            *landed,
            pltpu.SemaphoreType.DMA((len(plans) * nbits,)),
            pltpu.SemaphoreType.DMA((len(plans) * nbits,)),
        ],
        compiler_params=pltpu.CompilerParams(
            collective_id=1, has_side_effects=True, vmem_limit_bytes=56 << 20
        ),
    )(*operands)


def per_device(
    unit_ids, durations, unit_table, pre_weight, up_weight, post_weight, disc_taps, disc_out
):
    devices = lax.axis_size("tm")
    total_frames = F_DEV * devices
    total_samples = UP * total_frames
    matrices = disc_matrices(disc_taps, disc_out)
    gathered = gather_all(jnp.stack([unit_ids.reshape(-1, 128), durations.reshape(-1, 128)]), devices)
    frame_ids = frame_ids_of(gathered, total_frames)
    wave, wave_grad, grad_pre, grad_up = step(
        frame_ids, unit_table, pre_weight, up_weight, post_weight, matrices, devices
    )
    mean_scale = 1.0 / total_samples
    both = jnp.stack([wave, wave_grad])[:, :UP, HALO : HALO + F_DEV]
    both = both.transpose(0, 2, 1).reshape(2, -1)
    return (both[0], both[1], grad_pre * mean_scale, grad_up * mean_scale)


def solution(mesh):
    in_specs = (P(("groups", "tm")), P(("groups", "tm")), P(), P(), P(), P(), P(), P())
    out_specs = (
        P(("groups", "tm")),
        P(("groups", "tm")),
        P(("groups", "tm"), None),
        P(("groups", "tm"), None),
    )
    return jax.shard_map(
        per_device, mesh=mesh, in_specs=in_specs, out_specs=out_specs, check_vma=False
    )
```

```python
import functools

import jax
import jax.numpy as jnp
import numpy as np
from jax import lax
from jax.experimental import pallas as pl
from jax.experimental.pallas import tpu as pltpu
from jax.sharding import PartitionSpec as P

C = 256
UP = 5
KD = 5
F_DEV = 1536
HALO = 16
EXT = F_DEV + 2 * HALO
FRONT = 224
BACK = 256
LANES = 1664
CHUNK = 128
TURNS = 10
PAIRS = 32
CHANNELS = 160

period_list = (2, 3, 5, 7, 11)
log_two = 0.6931471805599453
MESH = pl.DeviceIdType.MESH
VMEM = pltpu.VMEM


def leaky_relu(v):
    return 0.1 * v + 0.9 * (jnp.maximum(v, 0.0) + jnp.log(1.0 + jnp.exp(-jnp.abs(v))) - log_two)


def leaky_slope(v):
    return 0.55 + 0.45 * jnp.tanh(0.5 * v)


def at_device(group, index):
    return (group, index)


def gather_kernel(n, x_ref, o_ref, send_sem, recv_sem):
    group = lax.axis_index("groups")
    me = lax.axis_index("tm")
    barrier = pltpu.get_barrier_semaphore()

    def greet(i, carry):
        pl.semaphore_signal(
            barrier, inc=1, device_id=at_device(group, (me + i) % n), device_id_type=MESH
        )
        return carry

    lax.fori_loop(1, n, greet, 0)
    pl.semaphore_wait(barrier, n - 1)

    def copy_to(i):
        return pltpu.make_async_remote_copy(
            src_ref=x_ref,
            dst_ref=o_ref.at[me],
            send_sem=send_sem.at[i],
            recv_sem=recv_sem.at[i],
            device_id=at_device(group, (me + i) % n),
            device_id_type=MESH,
        )

    def copy_from(i):
        source = (me + n - i) % n
        return pltpu.make_async_remote_copy(
            src_ref=x_ref,
            dst_ref=o_ref.at[source],
            send_sem=send_sem.at[i],
            recv_sem=recv_sem.at[i],
            device_id=at_device(group, (me + i) % n),
            device_id_type=MESH,
        )

    def send(i, carry):
        copy_to(i).start()
        return carry

    lax.fori_loop(1, n, send, 0)
    o_ref[me] = x_ref[...]

    def finish(i, carry):
        copy_from(i).wait()
        return carry

    lax.fori_loop(1, n, finish, 0)


def gather_all(x, n):
    return pl.pallas_call(
        functools.partial(gather_kernel, n),
        out_shape=jax.ShapeDtypeStruct((n,) + x.shape, x.dtype),
        in_specs=[pl.BlockSpec(memory_space=VMEM)],
        out_specs=pl.BlockSpec(memory_space=VMEM),
        scratch_shapes=[pltpu.SemaphoreType.DMA((n,)), pltpu.SemaphoreType.DMA((n,))],
        compiler_params=pltpu.CompilerParams(collective_id=0, has_side_effects=True),
    )(x)


def stream_plan(nbits, order):
    left = list(range(nbits))[::-1]
    plan = []
    for bit in order:
        place = left.index(bit)
        plan.append((bit, 2**place, 2 ** (len(left) - place - 1)))
        left.remove(bit)
    return plan


def stream_plans(n):
    nbits = n.bit_length() - 1
    first = tuple(range(nbits))
    second = (0,) + tuple(range(2, nbits)) + (1,)
    orders = [first, second] + [first] * 5
    return nbits, [stream_plan(nbits, order) for order in orders]


class Halving:
    def __init__(self, n, outs, targets, terms, held, landed, send_sem, recv_sem):
        self.nbits, self.plans = stream_plans(n)
        self.outs, self.targets, self.terms = outs, targets, terms
        self.held, self.landed = held, landed
        self.send_sem, self.recv_sem = send_sem, recv_sem
        self.group, me = lax.axis_index("groups"), lax.axis_index("tm")
        self.bits = [(me // 2**b) % 2 for b in range(self.nbits)]
        self.mates = [me + (1 - 2 * self.bits[b]) * 2**b for b in range(self.nbits)]

    def greet(self):
        barrier = pltpu.get_barrier_semaphore()
        for mate in self.mates:
            pl.semaphore_signal(
                barrier, inc=1, device_id=at_device(self.group, mate), device_id_type=MESH
            )

    def meet(self):
        pl.semaphore_wait(pltpu.get_barrier_semaphore(), self.nbits)

    def source(self, s, t):
        return self.terms[s] if t == 0 else self.held[s * (self.nbits - 1) + t - 1]

    def copy(self, s, t):
        bit = self.plans[s][t][0]
        return pltpu.make_async_remote_copy(
            src_ref=self.source(s, t).at[:, 1 - self.bits[bit]],
            dst_ref=self.landed[s * self.nbits + t],
            send_sem=self.send_sem.at[s * self.nbits + t],
            recv_sem=self.recv_sem.at[s * self.nbits + t],
            device_id=at_device(self.group, self.mates[bit]),
            device_id_type=MESH,
        )

    def put(self, s, term):
        ref = self.terms[s]
        ref[...] = term.reshape(ref.shape)
        self.copy(s, 0).start()

    def advance(self, s, t):
        self.copy(s, t).wait_recv()
        bit, hi, lo = self.plans[s][t]
        mine = self.bits[bit]
        here, there = self.source(s, t), self.landed[s * self.nbits + t]
        if t == self.nbits - 1:
            which, column = self.targets[s]
            self.outs[which][:, column : column + C] = here[0, mine, 0] + there[0, 0]
            return
        _, _, next_lo = self.plans[s][t + 1]
        onward = self.held[s * (self.nbits - 1) + t]
        for i in range(hi * lo):
            total = here[i // lo, mine, i % lo] + there[i // lo, i % lo]
            onward[i // (2 * next_lo), (i // next_lo) % 2, i % next_lo] = total
        self.copy(s, t + 1).start()

    def finish(self):
        for t in range(self.nbits):
            for s in range(len(self.plans)):
                self.copy(s, t).wait_send()


def unit_window(gathered, total_frames):
    n = gathered.shape[0]
    all_ids = gathered[:, 0].reshape(-1)
    dur_rows = gathered[:, 1].reshape(n, -1)
    row_units = dur_rows.shape[1]
    unit_iota = jnp.arange(row_units, dtype=jnp.int32)
    upper = (unit_iota[:, None] <= unit_iota[None, :]).astype(jnp.bfloat16)
    within = jnp.dot(dur_rows.astype(jnp.bfloat16), upper, preferred_element_type=jnp.float32)
    row_total = within[:, row_units - 1]
    offsets = jnp.cumsum(row_total) - row_total
    unit_ends = (within + offsets[:, None]).reshape(-1).astype(jnp.int32)
    start = lax.axis_index("tm") * F_DEV - HALO - 1
    far_end = jnp.full((LANES,), total_frames + LANES, jnp.int32)
    ends_padded = jnp.concatenate([unit_ends, far_end])
    ids_padded = jnp.concatenate([all_ids, jnp.zeros((LANES,), jnp.int32)])
    first_unit = jnp.sum((unit_ends <= start).astype(jnp.int32))
    window_ends = lax.dynamic_slice_in_dim(ends_padded, first_unit, LANES)
    window_ids = lax.dynamic_slice_in_dim(ids_padded, first_unit, LANES)
    return window_ends[None, :], window_ids[None, :]


def tap_places():
    reads = np.zeros((UP, 5, KD, TURNS * 8), np.float32)
    adds = np.zeros((TURNS * 8, UP * PAIRS), np.float32)
    for phase in range(UP):
        for r, period in enumerate(period_list):
            for k in range(KD):
                ahead = phase + k * period
                reads[phase, r, k, (ahead // UP) * 8 + ahead % UP] = 1.0
                behind = phase - k * period
                row = (-(behind // UP)) * 8 + phase
                adds[row, (behind % UP) * PAIRS + r * KD + k] = 1.0
    return reads, adds


def halves(x):
    high = x.astype(jnp.bfloat16)
    return high, (x - high.astype(jnp.float32)).astype(jnp.bfloat16)


def disc_matrices(disc_taps, disc_out):
    reads, adds = tap_places()
    spread = jnp.sum(disc_taps[None, :, :, :, None] * reads[:, :, :, None, :], axis=2)
    high, low = halves(spread.reshape(UP * CHANNELS, TURNS * 8))
    read_matrix = jnp.concatenate([high, high, low], axis=1)
    own = jnp.asarray(np.eye(5, dtype=np.float32))
    weighted = disc_taps * disc_out[:, None, :]
    repeated = jnp.broadcast_to(disc_out[:, None, :], disc_taps.shape)
    parts = []
    for x in (weighted, repeated):
        full = (x[:, :, None, :] * own[:, None, :, None]).reshape(25, CHANNELS)
        full = jnp.concatenate([full, jnp.zeros((PAIRS - 25, CHANNELS), jnp.float32)], axis=0)
        parts.append(jnp.concatenate(halves(full), axis=0))
    add_matrix = jnp.asarray(np.concatenate([adds, adds], axis=1), jnp.bfloat16)
    return read_matrix, parts[0], parts[1], add_matrix


def split_dot(matrix, x):
    high, low = halves(x)
    both = jnp.dot(matrix, high, preferred_element_type=jnp.float32)
    rest = jnp.dot(matrix[:PAIRS], low, preferred_element_type=jnp.float32)
    return both[:PAIRS] + both[PAIRS:] + rest


def step_kernel(
    devices,
    ends_ref,
    ids_ref,
    table_ref,
    pre_w,
    up_w,
    post_ref,
    read_ref,
    weighted_ref,
    repeated_ref,
    add_ref,
    wave_o,
    wave_grad_o,
    grad_pre_o,
    grad_up_o,
    rows,
    window,
    pre_out,
    pre_act,
    up_out,
    columns,
    wave,
    shifted,
    sums,
    up_grad,
    pre_grad,
    window_t,
    act_t,
    *stream_refs,
):
    nbits, plans = stream_plans(devices)
    count = len(plans)
    terms, stream_refs = stream_refs[:count], stream_refs[count:]
    held, stream_refs = stream_refs[: count * (nbits - 1)], stream_refs[count * (nbits - 1) :]
    landed, sems = stream_refs[: count * nbits], stream_refs[count * nbits :]
    targets = [(1, C * j) for j in range(UP)] + [(0, 0), (0, C)]
    halving = Halving(devices, (grad_pre_o, grad_up_o), targets, terms, held, landed, *sems)
    halving.greet()
    total_frames = devices * F_DEV
    first_frame = lax.axis_index("tm") * F_DEV - HALO
    vocab = table_ref.shape[0]

    ends = ends_ref[...]
    slot = lax.broadcasted_iota(jnp.int32, (1, LANES), 1)
    starts = jnp.where(slot == 0, -LANES, pltpu.roll(ends, 1, 1))

    def embed(i, carry):
        at = pl.multiple_of(i * FRONT, FRONT)
        row = lax.broadcasted_iota(jnp.int32, (FRONT, 1), 0)
        position = row + (at + first_frame - 1)
        owned = (starts <= position) & (position < ends)
        ids = jnp.sum(jnp.where(owned, ids_ref[...], 0).astype(jnp.float32), axis=1, keepdims=True)
        known = (position >= 0) & (position < total_frames)
        ids = jnp.where(known, ids, -1.0)
        places = lax.broadcasted_iota(jnp.int32, (FRONT, vocab), 1).astype(jnp.float32)
        one_hot = (ids == places).astype(jnp.bfloat16)
        rows[pl.ds(at, FRONT), :] = jnp.dot(
            one_hot, table_ref[...], preferred_element_type=jnp.float32
        )
        return carry

    lax.fori_loop(0, rows.shape[0] // FRONT, embed, 0)

    columns[pl.ds(EXT, LANES - EXT), :] = jnp.zeros((LANES - EXT, 128), jnp.float32)
    lane = lax.broadcasted_iota(jnp.int32, (FRONT, 128), 1)
    for i in range(EXT // FRONT):
        at = i * FRONT
        taps = [rows[at + k : at + k + FRONT, :].astype(jnp.bfloat16) for k in range(3)]
        win = jnp.concatenate(taps, axis=1)
        window[at : at + FRONT, :] = win
        pre = jnp.dot(win, pre_w[...], preferred_element_type=jnp.float32).astype(jnp.bfloat16)
        pre_out[at : at + FRONT, :] = pre
        act = leaky_relu(pre.astype(jnp.float32)).astype(jnp.bfloat16)
        pre_act[at : at + FRONT, :] = act
        column = jnp.zeros((FRONT, 128), jnp.float32)
        for j in range(UP):
            up = jnp.dot(
                act, up_w[:, C * j : C * (j + 1)], preferred_element_type=jnp.float32
            ).astype(jnp.bfloat16)
            up_out[at : at + FRONT, C * j : C * (j + 1)] = up
            terms = leaky_relu(up.astype(jnp.float32)) * post_ref[...]
            column = jnp.where(lane == j, jnp.sum(terms, axis=1, keepdims=True), column)
        columns[at : at + FRONT, :] = column

    frame = lax.broadcasted_iota(jnp.int32, (8, LANES), 1) + first_frame
    for b in range(LANES // 128):
        at = 128 * b
        wave[:, at : at + 128] = columns[at : at + 128, :].T[:8, :]
    inside = (frame >= 0) & (frame < total_frames)
    signal = jnp.where(inside, jnp.tanh(wave[...]), 0.0)
    wave[...] = signal
    depth = TURNS * 8
    for q in range(0, TURNS, 2):
        turned = [signal if t == 0 else pltpu.roll(signal, LANES - t, 1) for t in (q, q + 1)]
        high, low = halves(jnp.concatenate(turned, axis=0))
        shifted[8 * q : 8 * q + 16, :] = high
        shifted[depth + 8 * q : depth + 8 * q + 16, :] = low
        shifted[2 * depth + 8 * q : 2 * depth + 8 * q + 16, :] = high

    chunk_lane = lax.broadcasted_iota(jnp.int32, (PAIRS, CHUNK), 1)

    def judge(i, carry):
        at = pl.multiple_of(i * CHUNK, CHUNK)
        real = chunk_lane + (at + first_frame) >= 0
        taps = shifted[:, pl.ds(at, CHUNK)]
        highs, lows = [], []
        for j in range(UP):
            pre = jnp.dot(
                read_ref[CHANNELS * j : CHANNELS * (j + 1), :],
                taps,
                preferred_element_type=jnp.float32,
            )
            scores = split_dot(repeated_ref[...], leaky_relu(pre))
            adjoint = split_dot(weighted_ref[...], leaky_slope(pre)) * (scores - 1.0)
            high, low = halves(jnp.where(real, adjoint, 0.0))
            highs.append(high)
            lows.append(low)
        sums[:, pl.ds(at, CHUNK)] = jnp.dot(
            add_ref[...], jnp.concatenate(highs + lows, axis=0), preferred_element_type=jnp.float32
        )
        return carry

    lax.fori_loop(0, LANES // CHUNK, judge, 0)
    wave_grad = sums[0:8, :]
    for q in range(1, TURNS):
        wave_grad = wave_grad + pltpu.roll(sums[8 * q : 8 * q + 8, :], q, 1)
    wave_o[...] = signal
    wave_grad_o[...] = wave_grad
    sums[0:8, :] = wave_grad * (1.0 - signal * signal)
    for b in range(LANES // 128):
        at = 128 * b
        columns[at : at + 128, 0:8] = sums[0:8, at : at + 128].T

    blocks = [(i * BACK, i * BACK + HALO) for i in range(F_DEV // BACK)]
    for to, at in blocks:
        act_t[:, to : to + BACK] = pre_act[at : at + BACK, :].T
        window_t[:, to : to + BACK] = window[at : at + BACK, :].T
    halving.meet()
    for j in range(UP):
        for to, at in blocks:
            slope = leaky_slope(up_out[at : at + BACK, C * j : C * (j + 1)].astype(jnp.float32))
            grad = columns[at : at + BACK, j : j + 1] * post_ref[...] * slope
            up_grad[to : to + BACK, C * j : C * (j + 1)] = grad.astype(jnp.bfloat16)
        term = jnp.dot(
            act_t[...], up_grad[:, C * j : C * (j + 1)], preferred_element_type=jnp.float32
        )
        halving.put(j, term)
        if j > 0:
            halving.advance(j - 1, 0)
    for to, at in blocks:
        hidden = lax.dot_general(
            up_grad[to : to + BACK, :],
            up_w[...],
            (((1,), (1,)), ((), ())),
            preferred_element_type=jnp.float32,
        )
        slope = leaky_slope(pre_out[at : at + BACK, :].astype(jnp.float32))
        pre_grad[to : to + BACK, :] = (hidden * slope).astype(jnp.bfloat16)
    halving.advance(UP - 1, 0)
    halving.advance(0, 1)
    halving.advance(1, 1)
    for j in range(2):
        term = jnp.dot(
            window_t[...], pre_grad[:, C * j : C * (j + 1)], preferred_element_type=jnp.float32
        )
        halving.put(UP + j, term)
    halving.advance(UP, 0)
    halving.advance(UP + 1, 0)
    for t in range(1, nbits):
        for s in range(2 if t == 1 else 0, count):
            halving.advance(s, t)
    halving.finish()


def step(units, unit_table, pre_weight, up_weight, post_weight, matrices, devices):
    width, depth, span = up_weight.shape[1], up_weight.shape[0], pre_weight.shape[0]
    shape, bf16, f32 = jax.ShapeDtypeStruct, jnp.bfloat16, jnp.float32
    operands = (*units, unit_table, pre_weight, up_weight, post_weight[None, :], *matrices)
    nbits, plans = stream_plans(devices)
    terms, held, landed = [], [], []
    for s, plan in enumerate(plans):
        rows = (depth if s < UP else span) // devices
        for t, (_, hi, lo) in enumerate(plan):
            (held if t > 0 else terms).append(VMEM((hi, 2, lo, rows, C), f32))
            landed.append(VMEM((hi, lo, rows, C), f32))
    return pl.pallas_call(
        functools.partial(step_kernel, devices),
        out_shape=[
            shape((8, LANES), f32),
            shape((8, LANES), f32),
            shape((span // devices, depth), f32),
            shape((depth // devices, width), f32),
        ],
        in_specs=[pl.BlockSpec(memory_space=VMEM)] * len(operands),
        out_specs=[pl.BlockSpec(memory_space=VMEM)] * 4,
        scratch_shapes=[
            VMEM((FRONT * (EXT // FRONT + 1), unit_table.shape[1]), f32),
            VMEM((EXT, span), bf16),
            VMEM((EXT, depth), bf16),
            VMEM((EXT, depth), bf16),
            VMEM((EXT, width), bf16),
            VMEM((LANES, 128), f32),
            VMEM((8, LANES), f32),
            VMEM((3 * TURNS * 8, LANES), bf16),
            VMEM((TURNS * 8, LANES), f32),
            VMEM((F_DEV, width), bf16),
            VMEM((F_DEV, depth), bf16),
            VMEM((span, F_DEV), bf16),
            VMEM((depth, F_DEV), bf16),
            *terms,
            *held,
            *landed,
            pltpu.SemaphoreType.DMA((len(plans) * nbits,)),
            pltpu.SemaphoreType.DMA((len(plans) * nbits,)),
        ],
        compiler_params=pltpu.CompilerParams(
            collective_id=1, has_side_effects=True, vmem_limit_bytes=56 << 20
        ),
    )(*operands)


def per_device(
    unit_ids, durations, unit_table, pre_weight, up_weight, post_weight, disc_taps, disc_out
):
    devices = lax.axis_size("tm")
    total_frames = F_DEV * devices
    total_samples = UP * total_frames
    matrices = disc_matrices(disc_taps, disc_out)
    gathered = gather_all(jnp.stack([unit_ids.reshape(-1, 128), durations.reshape(-1, 128)]), devices)
    units = unit_window(gathered, total_frames)
    wave, wave_grad, grad_pre, grad_up = step(
        units, unit_table, pre_weight, up_weight, post_weight, matrices, devices
    )
    mean_scale = 1.0 / total_samples
    both = jnp.stack([wave, wave_grad])[:, :UP, HALO : HALO + F_DEV]
    both = both.transpose(0, 2, 1).reshape(2, -1)
    return (both[0], both[1], grad_pre * mean_scale, grad_up * mean_scale)


def solution(mesh):
    in_specs = (P(("groups", "tm")), P(("groups", "tm")), P(), P(), P(), P(), P(), P())
    out_specs = (
        P(("groups", "tm")),
        P(("groups", "tm")),
        P(("groups", "tm"), None),
        P(("groups", "tm"), None),
    )
    return jax.shard_map(
        per_device, mesh=mesh, in_specs=in_specs, out_specs=out_specs, check_vma=False
    )
```
